32 devices in a mesh: section: 4 (over x, core), ex: 2 (over y), tp: 4 (over z).
Axes of the slice: x: 2, y: 2, z: 4, core: 2. Of those that a mesh axis runs over, the one named last changes fastest.
Arguments:
- clean_heads: bfloat16 [4, 2, 512, 4096], P('section', 'ex', None, 'tp'), may hold values from -6 to 6
- corrupt_heads: bfloat16 [4, 2, 512, 4096], P('section', 'ex', None, 'tp'), may hold values from -6 to 6
- donors: int32 [512, 2], P('ex'), may hold values from 0 to 1, each once within a row
- senders: int32 [4, 8], P('section', 'tp'), may hold values from 0 to 31, as said below
- out_weight: bfloat16 [4, 4096, 8192], P('section', 'tp', 'ex'), may hold values from -0.1875 to 0.1875
- residual: bfloat16 [4, 2, 512, 8192], P('section', 'ex', None, 'tp'), may hold values from -160 to 160
- norm_gain: bfloat16 [4, 8192], P('section', 'tp'), may hold values from 0.25 to 1.75
- value_weight: bfloat16 [4, 8192, 1024], P('section', 'tp', 'ex'), may hold values from -0.0625 to 0.0625
- clean_values: bfloat16 [4, 2, 512, 1024], P('section', 'ex', None, 'tp'), may hold values from -6 to 6
- queries: bfloat16 [4, 2, 512, 4096], P('section', 'ex', None, 'tp'), may hold values from -120 to 120
- key_vectors: bfloat16 [4, 2, 512, 1024], P('section', 'ex', None, 'tp'), may hold values from -4 to 4
- receivers: int32 [4, 32], P('section', 'tp'), may hold values 0 or 1
Outputs:
- attended: bfloat16 [4, 2, 512, 4096], P('section', 'ex', None, 'tp')
The draws below stay inside these ranges and needn't reach their ends.
Inputs may be any that keep to these rules, and one draw needn't show every extreme that they name: `donors`: each position's row is a permutation of the 2 examples. `senders`: in each section's row, entries j * 2 to (j + 1) * 2 - 1 are distinct heads of j * 8 to (j + 1) * 8 - 1.
All inputs are finite; a program needn't handle non-finite values. No bound on the sum of `receivers` on one device may be relied on, other than what follows from the above.
Results may differ from the reference program's by a relative error of at most 0.012.
Values may be sent and summed in bfloat16 or wider, within the bound.
No kernel may reach another device: no remote copies, remote signals or barrier semaphores. Data moves between devices by JAX's collectives and lax.ppermute only.
A program may use at most 128 MiB of HBM per device.

```python
import math
import jax
import jax.numpy as jnp
from jax import lax

D = 8192
KVH = 8
HD = 128
HEADS = 32
GROUP = 4
SEND_DEV = 2
SEQ = 512
SECTIONS = 4
EXAMPLES = 2
SENDERS = 8
QHEADS = 32
N_TP = 4


def pair_draw(key):
    key_one, key_two = jax.random.split(key, 2)
    key_vectors = jnp.clip(jax.random.normal(key_one, (SECTIONS, EXAMPLES, SEQ, KVH, HD), jnp.float32), -4.0, 4.0)
    queries = jnp.clip(jax.random.normal(key_two, (SECTIONS, EXAMPLES, SEQ, KVH, GROUP, HD), jnp.float32), -4.0, 4.0)
    return (queries.reshape(SECTIONS, EXAMPLES, SEQ, KVH * GROUP * HD), key_vectors.reshape(SECTIONS, EXAMPLES, SEQ, KVH * HD))


def draw_queries(key, part):
    return pair_draw(jax.random.fold_in(key, 11))[0].astype(jnp.bfloat16)


def draw_key_vectors(key, part):
    return pair_draw(jax.random.fold_in(key, 11))[1].astype(jnp.bfloat16)


def draw_residual(key, part):
    key_one, key_two = jax.random.split(key, 2)
    shape = (SECTIONS, EXAMPLES, SEQ, D)
    rising = 3.0 ** (jnp.arange(D, dtype=jnp.float32) / D)
    spread = jnp.exp(jax.random.uniform(key_one, (SECTIONS, 1, 1, D), jnp.float32, 0.0, math.log(3.0)))
    sampled = jnp.clip(jax.random.normal(key_two, shape, jnp.float32), -6.0, 6.0)
    return (sampled * rising * spread).astype(jnp.bfloat16)


def draw_senders(key, part):
    blocks = SENDERS // SEND_DEV
    per_block = HEADS // blocks
    stream_keys = jax.random.split(jax.random.fold_in(key, 5), SECTIONS * blocks)
    chosen_heads = jax.vmap(lambda single: jax.random.permutation(single, per_block)[:SEND_DEV])(stream_keys)
    offsets = jnp.arange(SECTIONS * blocks) % blocks * per_block
    return (chosen_heads + offsets[:, None]).reshape(SECTIONS, SENDERS).astype(jnp.int32)


def touch_ends(result, rng, low, top_value):
    longest = result.shape.index(max(result.shape))
    spots = []
    for shift in (0, 1):
        where = [jax.random.randint(jax.random.fold_in(rng, axis), (), 0, length) for axis, length in enumerate(result.shape)]
        where[longest] = (where[longest] + shift) % result.shape[longest]
        spots.append(tuple(where))
    return result.at[spots[0]].set(low).at[spots[1]].set(top_value)


def shard_levels(key, shape, cuts, smallest, largest):
    level = 1.0
    for dim, shards_of in cuts:
        steps = jax.random.uniform(jax.random.fold_in(jax.random.fold_in(key, 6), dim), (shards_of,), jnp.float32, smallest / len(cuts), largest / len(cuts))
        level = level * jnp.repeat(jnp.exp(steps), shape[dim] // shards_of).reshape((-1,) + (1,) * (len(shape) - 1 - dim))
    return level


def normal_values(key, extent, deviation, most, cuts=(), held_as=jnp.bfloat16):
    drawn = jax.random.normal(key, extent, jnp.float32) * deviation
    if len(cuts) > 0:
        drawn = shard_levels(key, extent, cuts, -0.22, 0.18) * drawn
    return jnp.clip(drawn, min=-most, max=most).astype(held_as)


def setup_inputs(seed: int = 0) -> dict:
    seeds = jax.random.split(jax.random.key(seed), 13)
    clean_heads = normal_values(seeds[0], (SECTIONS, EXAMPLES, SEQ, HEADS * HD), 1.0, 6.0, ((0, 4), (1, 2), (3, 4)))
    corrupt_heads = normal_values(seeds[1], (SECTIONS, EXAMPLES, SEQ, HEADS * HD), 1.0, 6.0, ((0, 4), (1, 2), (3, 4)))
    donors = jax.vmap(lambda own: jax.random.permutation(own, EXAMPLES))(jax.random.split(seeds[2], SEQ)).reshape((SEQ, EXAMPLES)).astype(jnp.int32)
    senders = draw_senders(jax.random.fold_in(seeds[12], 71), 0)
    out_weight = normal_values(seeds[4], (SECTIONS, HEADS * HD, D), (SENDERS * HD) ** -0.5, 0.1875, ((0, 4), (1, 4), (2, 2)))
    residual = draw_residual(jax.random.fold_in(seeds[12], 71), 0)
    norm_gain = jnp.clip(1.0 + 0.15 * jax.random.normal(seeds[6], (SECTIONS, D), jnp.float32), 0.25, 1.75).astype(jnp.bfloat16)
    value_weight = normal_values(seeds[7], (SECTIONS, D, KVH * HD), D ** -0.5, 0.0625, ((0, 4), (1, 4), (2, 2)))
    clean_values = normal_values(seeds[8], (SECTIONS, EXAMPLES, SEQ, KVH * HD), 1.0, 6.0, ((0, 4), (1, 2), (3, 4)))
    queries = draw_queries(jax.random.fold_in(seeds[12], 71), 0)
    key_vectors = draw_key_vectors(jax.random.fold_in(seeds[12], 71), 0)
    receivers = touch_ends((jax.random.randint(seeds[11], (SECTIONS, QHEADS), 0, 2) < 1).astype(jnp.int32), jax.random.fold_in(seeds[11], 1), 0, 1)
    return {"clean_heads": clean_heads, "corrupt_heads": corrupt_heads, "donors": donors, "senders": senders, "out_weight": out_weight, "residual": residual, "norm_gain": norm_gain, "value_weight": value_weight, "clean_values": clean_values, "queries": queries, "key_vectors": key_vectors, "receivers": receivers}


def rounded(values):
    return lax.optimization_barrier(values.astype(jnp.bfloat16)).astype(jnp.float32)

def attend(queries, key_vectors, chosen):
    scores = jnp.einsum('etkgd,eukd->ekgtu', queries.astype(jnp.float32), key_vectors.astype(jnp.float32))
    scores = scores * (1.0 / math.sqrt(HD))
    places = jnp.arange(scores.shape[-1])
    causal = places[:, None] >= places[None, :]
    scores = jnp.where(causal, scores, -jnp.inf)
    maxima = lax.optimization_barrier(jnp.max(scores, axis=-1, keepdims=True))
    exponent = jnp.exp(scores - maxima)
    weights = (exponent / lax.optimization_barrier(jnp.sum(exponent, axis=-1, keepdims=True))).astype(jnp.bfloat16)
    return jnp.einsum('ekgtu,eukgd->etkgd', weights.astype(jnp.float32), chosen.astype(jnp.float32))

def reference(clean_heads, corrupt_heads, donors, senders, out_weight, residual, norm_gain, value_weight, clean_values, queries, key_vectors, receivers):
    examples, length = (residual.shape[1], residual.shape[2])
    row_count = examples * length
    width_tp = D // N_TP
    positions = jnp.arange(length)
    carried = jnp.zeros((row_count, D), jnp.float32)
    results = []
    for which_section in range(SECTIONS):
        patched = corrupt_heads[which_section][donors.T, positions[None, :], :]
        difference = patched.astype(jnp.float32) - clean_heads[which_section].astype(jnp.float32)
        difference = difference.reshape(row_count, HEADS, HD)
        head_rows = out_weight[which_section].reshape(HEADS, HD, D)
        increment = jnp.zeros((row_count, D), jnp.float32)
        for which_block in range(N_TP):
            chosen_heads = senders[which_section, which_block * SEND_DEV:(which_block + 1) * SEND_DEV]
            picked = jnp.take(difference, chosen_heads, axis=1).astype(jnp.bfloat16).reshape(row_count, SEND_DEV * HD)
            sender_rows = jnp.take(head_rows, chosen_heads, axis=0).reshape(SEND_DEV * HD, D)
            increment = increment + rounded(jnp.dot(picked, sender_rows, preferred_element_type=jnp.float32))
        carried = carried + increment
        stream = residual[which_section].reshape(row_count, D).astype(jnp.float32) + carried
        scale = lax.rsqrt(lax.optimization_barrier(jnp.mean(stream * stream, axis=-1, keepdims=True)) + 1e-05)
        normed = (stream * scale * norm_gain[which_section].astype(jnp.float32)).astype(jnp.bfloat16)
        values = jnp.zeros((row_count, KVH * HD), jnp.float32)
        for which_block in range(N_TP):
            lower = which_block * width_tp
            values = values + rounded(jnp.dot(normed[:, lower:lower + width_tp], value_weight[which_section, lower:lower + width_tp], preferred_element_type=jnp.float32))
        values = values.astype(jnp.bfloat16).reshape(examples, length, KVH, 1, HD)
        clean_here = clean_values[which_section].reshape(examples, length, KVH, 1, HD)
        receive_flags = receivers[which_section].reshape(KVH, GROUP)
        chosen = jnp.where((receive_flags == 1)[None, None, :, :, None], values, clean_here)
        attended = attend(queries[which_section].reshape(examples, length, KVH, GROUP, HD), key_vectors[which_section].reshape(examples, length, KVH, HD), chosen)
        results.append(attended.reshape(examples, length, KVH * GROUP * HD).astype(jnp.bfloat16))
    return jnp.stack(results)
```

```python
import functools
import math

import jax
import jax.numpy as jnp
from jax import lax
from jax.experimental import pallas as pl
from jax.experimental.pallas import tpu as pltpu
from jax.sharding import PartitionSpec as P

CHUNKS = 2
F32 = jnp.float32
BF16 = jnp.bfloat16


def ring(size, shift):
    return [(i, (i + shift) % size) for i in range(size)]


def line(size, shift):
    return [(i, i + shift) for i in range(size) if 0 <= i + shift < size]


def pick_heads(ids, corrupt, clean, head):
    count = ids.shape[0]
    length = corrupt.shape[0]

    def body(ids_ref, corrupt_ref, clean_ref, corrupt_out, clean_out, sems):
        copies = []
        for which, (src, dst) in enumerate(((corrupt_ref, corrupt_out), (clean_ref, clean_out))):
            for h in range(count):
                start = pl.multiple_of(ids_ref[h] * head, head)
                copies.append(
                    pltpu.make_async_copy(
                        src.at[:, pl.ds(start, head)],
                        dst.at[:, pl.ds(h * head, head)],
                        sems.at[which * count + h],
                    )
                )
        for copy in copies:
            copy.start()
        for copy in copies:
            copy.wait()

    shape = jax.ShapeDtypeStruct((length, count * head), corrupt.dtype)
    return pl.pallas_call(
        body,
        out_shape=(shape, shape),
        in_specs=[
            pl.BlockSpec(memory_space=pltpu.SMEM),
            pl.BlockSpec(memory_space=pl.ANY),
            pl.BlockSpec(memory_space=pl.ANY),
        ],
        out_specs=[pl.BlockSpec(memory_space=pltpu.VMEM)] * 2,
        scratch_shapes=[pltpu.SemaphoreType.DMA((2 * count,))],
        name="pick_heads",
    )(ids, corrupt, clean)


def pick_rows(ids, units, weight, head, width, chunks, parts, per_part):
    count = ids.shape[0]
    part_width = width // chunks

    def body(ids_ref, units_ref, weight_ref, *rest):
        outs, sems = rest[:-1], rest[-1]
        copies = []
        for c in range(chunks):
            for d in range(parts):
                for m in range(per_part):
                    for h in range(count):
                        row = pl.multiple_of(ids_ref[h] * head, head)
                        column = pl.multiple_of(
                            units_ref[d * per_part + m] * width + c * part_width, part_width
                        )
                        copies.append(
                            pltpu.make_async_copy(
                                weight_ref.at[pl.ds(row, head), pl.ds(column, part_width)],
                                outs[c * parts + d].at[pl.ds((m * count + h) * head, head), :],
                                sems.at[len(copies)],
                            )
                        )
        for copy in copies:
            copy.start()
        for copy in copies:
            copy.wait()

    shape = jax.ShapeDtypeStruct((per_part * count * head, part_width), weight.dtype)
    total = chunks * parts
    return pl.pallas_call(
        body,
        out_shape=(shape,) * total,
        in_specs=[
            pl.BlockSpec(memory_space=pltpu.SMEM),
            pl.BlockSpec(memory_space=pltpu.SMEM),
            pl.BlockSpec(memory_space=pl.ANY),
        ],
        out_specs=[pl.BlockSpec(memory_space=pltpu.VMEM)] * total,
        scratch_shapes=[pltpu.SemaphoreType.DMA((total * per_part * count,))],
        name="pick_rows",
    )(ids, units, weight)


def earlier_sections(own, axis, size):
    place = lax.axis_index(axis)
    if size & (size - 1):
        total = jnp.zeros_like(own)
        for d in range(1, size):
            total += lax.ppermute(own.astype(BF16), axis, line(size, d)).astype(F32)
        return total
    rows = own.shape[0]
    before = None
    group = own
    span = 1
    while span < size:
        last = span * 2 >= size
        low = [(i, i + span) for i in range(size) if not i & span]
        pairs = low if last and span > 1 else [(i, i ^ span) for i in range(size)]
        piece = group.astype(BF16)
        if span > 1:
            piece = lax.dynamic_slice_in_dim(piece, (place % span) * (rows // span), rows // span, 0)
        piece = lax.ppermute(piece, axis, pairs)
        step = 1
        while step < span:
            other = lax.ppermute(piece, axis, [(i, i ^ step) for i in range(size)])
            upper = (place & step) > 0
            piece = jnp.concatenate([jnp.where(upper, other, piece), jnp.where(upper, piece, other)])
            step *= 2
        piece = piece.astype(F32)
        add = jnp.where((place & span) > 0, piece, 0.0)
        before = add if before is None else before + add
        group = group + piece
        span *= 2
    return jnp.zeros_like(own) if before is None else before


def per_device(
    sizes,
    clean_heads,
    corrupt_heads,
    donors,
    senders,
    out_weight,
    residual,
    norm_gain,
    value_weight,
    clean_values,
    queries,
    key_vectors,
    receivers,
):
    sections, parts, ranks = sizes
    e = lax.axis_index("ex")
    j = lax.axis_index("tp")
    length = residual.shape[2]
    block = residual.shape[3]
    features = block * ranks
    width = block // parts
    heads_q = receivers.shape[1]
    head = queries.shape[3] // heads_q
    kv_here = key_vectors.shape[3] // head
    group = heads_q // kv_here
    heads_here = clean_heads.shape[3] // head
    chunks = CHUNKS if width % (CHUNKS * head) == 0 else 1
    part_width = width // chunks
    ids = senders[0] - j * heads_here
    count = ids.shape[0]
    channels = count * head

    corrupt, clean = pick_heads(ids, corrupt_heads[0, 0], clean_heads[0, 0], head)
    spread = donors.shape[0]
    donor_rows = donors.T
    own_donors = jnp.zeros((length,), donors.dtype)
    patched = None
    pieces = [corrupt]
    for d in range(1, parts):
        pieces.append(lax.ppermute(corrupt, "ex", ring(parts, d)))
    for d in range(parts):
        wanted = lax.dynamic_index_in_dim(donor_rows, (e + d) % parts, 0, keepdims=False)
        if d:
            wanted = lax.ppermute(wanted, "ex", ring(parts, d))
        own_donors = lax.dynamic_update_slice(own_donors, wanted, (((e - d) % parts) * spread,))
    for d in range(parts):
        take = (own_donors == (e - d) % parts)[:, None]
        patched = pieces[d] if patched is None else jnp.where(take, pieces[d], patched)
    difference = (patched.astype(F32) - clean.astype(F32)).astype(BF16)

    per_part = max(1, ranks // parts)
    units = []
    for d in range(parts):
        target = (e + d) % parts
        for m in range(per_part):
            units.append(jnp.minimum((target - e * ranks) % parts + parts * m, ranks - 1))
    units = jnp.stack(units).astype(jnp.int32)
    rows_cut = pick_rows(ids, units, out_weight[0], head, width, chunks, parts, per_part)
    projection = []
    for c in range(chunks):
        held = [rows_cut[c * parts]]
        for d in range(1, parts):
            held.append(lax.ppermute(rows_cut[c * parts + d], "ex", ring(parts, d)))
        held = jnp.stack(held).reshape(parts * per_part, channels, part_width)
        received = []
        for t in range(ranks):
            unit = ((j + t) % ranks) * parts + e
            index = ((e - unit // ranks) % parts) * per_part + (unit % ranks) // parts
            out = lax.dynamic_index_in_dim(held, index, 0, keepdims=False)
            received.append(lax.ppermute(out, "tp", ring(ranks, t)) if t else out)
        projection.append(jnp.concatenate(received))

    up, down = [difference], [difference]
    for t in range(1, ranks):
        up.append(lax.ppermute(up[-1], "tp", line(ranks, 1)))
        down.append(lax.ppermute(down[-1], "tp", line(ranks, -1)))
    gathered = [difference]
    for t in range(1, ranks):
        gathered.append(jnp.where(j >= t, up[t], down[ranks - t]))
    examples = [jnp.concatenate(gathered, axis=1)]
    for d in range(1, parts):
        examples.append(
            jnp.concatenate([lax.ppermute(g, "ex", ring(parts, d)) for g in gathered], axis=1)
        )
    every = jnp.concatenate(examples)

    def columns_of(array, axis):
        got = []
        for d in range(parts):
            out = lax.dynamic_slice_in_dim(array, ((e + d) % parts) * width, width, axis)
            got.append(lax.ppermute(out, "ex", ring(parts, d)) if d else out)
        return got

    stream0 = jnp.concatenate(columns_of(residual[0, 0], 1))
    weight_parts = jnp.stack(columns_of(value_weight[0], 0))
    order = (e - jnp.arange(parts)) % parts
    weight_parts = jnp.concatenate(
        [lax.dynamic_index_in_dim(weight_parts, order[p], 0, keepdims=False) for p in range(parts)],
        axis=1,
    )
    gain = lax.dynamic_slice_in_dim(norm_gain[0], e * width, width, 0).astype(F32)

    q = queries[0, 0].reshape(length, kv_here, group, head)
    k = key_vectors[0, 0].reshape(length, kv_here, head)
    scores = jnp.einsum("tkgd,ukd->kgtu", q, k, preferred_element_type=F32) * (1.0 / math.sqrt(head))
    places = jnp.arange(length)
    scores = jnp.where(places[:, None] >= places[None, :], scores, -jnp.inf)
    exponent = jnp.exp(scores - jnp.max(scores, axis=-1, keepdims=True))
    weights = (exponent / jnp.sum(exponent, axis=-1, keepdims=True)).astype(BF16)
    weights = lax.optimization_barrier(weights)

    squares = None
    scaled = []
    for c in range(chunks):
        increment = jnp.dot(every, projection[c], preferred_element_type=F32)
        carried = increment + earlier_sections(increment, "section", sections)
        cut = slice(c * part_width, (c + 1) * part_width)
        stream = stream0[:, cut].astype(F32) + carried
        part = jnp.sum(stream * stream, axis=-1)
        squares = part if squares is None else squares + part
        scaled.append((stream * gain[cut]).astype(BF16))
    scaled = jnp.concatenate(scaled, axis=1)

    columns = weight_parts.shape[1] // ranks
    summed = None
    for t in reversed(range(ranks)):
        target = (j + t) % ranks
        cut = lax.dynamic_slice_in_dim(weight_parts, target * columns, columns, 1)
        term = jnp.dot(scaled, cut, preferred_element_type=F32)
        mine = term[:length]
        for d in range(1, parts):
            out = term[d * length : (d + 1) * length].astype(BF16)
            mine = mine + lax.ppermute(out, "ex", ring(parts, -d)).astype(F32)
        if t:
            mine = lax.ppermute(mine.astype(BF16), "tp", ring(ranks, t)).astype(F32)
        summed = mine if summed is None else summed + mine
    mine = squares[:length]
    for d in range(1, parts):
        mine = mine + lax.ppermute(squares[d * length : (d + 1) * length], "ex", ring(parts, -d))
    total = mine
    for t in range(1, ranks):
        total = total + lax.ppermute(mine, "tp", ring(ranks, t))
    scale = lax.rsqrt(total / features + 1e-05)
    values = (summed * scale[:, None]).astype(BF16)

    values = values.reshape(length, kv_here, 1, head)
    clean_here = clean_values[0, 0].reshape(length, kv_here, 1, head)
    flags = receivers[0].reshape(kv_here, group)
    chosen = jnp.where((flags == 1)[None, :, :, None], values, clean_here)
    attended = jnp.einsum("kgtu,ukgd->tkgd", weights, chosen, preferred_element_type=F32)
    return attended.reshape(1, 1, length, -1).astype(BF16)


def solution(mesh):
    sizes = (mesh.shape["section"], mesh.shape["ex"], mesh.shape["tp"])
    return jax.shard_map(
        functools.partial(per_device, sizes),
        mesh=mesh,
        in_specs=(
            P("section", "ex", None, "tp"),
            P("section", "ex", None, "tp"),
            P("ex", None),
            P("section", "tp"),
            P("section", "tp", "ex"),
            P("section", "ex", None, "tp"),
            P("section", "tp"),
            P("section", "tp", "ex"),
            P("section", "ex", None, "tp"),
            P("section", "ex", None, "tp"),
            P("section", "ex", None, "tp"),
            P("section", "tp"),
        ),
        out_specs=P("section", "ex", None, "tp"),
        check_vma=False,
    )
```
